32 devices in a mesh: dp: 8 (over z, y), mp: 4 (over x, core).
Axes of the slice: x: 2, y: 2, z: 4, core: 2. Of those that a mesh axis runs over, the one named last changes fastest.
Arguments:
- latents: bfloat16 [262144, 256], P(('dp', 'mp')), may hold values from -6 to 6
- proj_weight: bfloat16 [18, 256], replicated, may hold values from -0.375 to 0.375
- proj_bias: float32 [18], replicated, may hold values from -2.5 to 2.5
- fill: int32 [2048], replicated, may hold values from 0 to 128, as said below
- target: int32 [2048], replicated, may hold values from -1 to 7, as said below
- target_slot: int32 [2048], replicated, may hold values from -1 to 31, as said below
Outputs:
- latent_grad: bfloat16 [131072, 256], P(('dp', 'mp'))
- weight_grad: float32 [18, 256], replicated
- entropy_loss: float32 [], replicated
The draws below stay inside these ranges and needn't reach their ends.
Inputs may be any that keep to these rules, and one draw needn't show every extreme that they name: `fill`: zero exactly on the empty slots of a device, which are those whose target is -1. `target`: blocks go to devices with the same mp index. Each device receives exactly 32 blocks, one in each of its positions; at most 8 blocks goes from one device to any one index of dp, and some device does send 8 block to an index. -1 marks an empty slot. `target_slot`: -1 exactly where target is -1.
All inputs are finite; a program needn't handle non-finite values.
Results may differ from the reference program's by a relative error of at most 0.0049.
Values may be sent and summed in bfloat16 or wider, within the bound.
A program may use at most 64 MiB of HBM per device.

```python
import jax
import jax.numpy as jnp
from jax import lax

D = 256
BITS = 18
BLK = 128
OUT_SLOTS = 32
IN_SLOTS = 64
NIN = 2048
N_DP = 8
N_MP = 4


def column_layout(key):
    subkeys = jax.random.split(key, 8)
    capacity = max(1, 2 * OUT_SLOTS // N_DP)
    paired = N_DP // 2
    spread = IN_SLOTS - OUT_SLOTS
    pairing = jax.random.permutation(subkeys[0], N_DP)
    surplus = jax.random.randint(subkeys[1], (paired,), -spread, spread + 1)
    surplus = surplus.at[0].set(spread)
    offsets = jnp.zeros((N_DP,), jnp.int32).at[pairing[:paired]].set(surplus).at[pairing[paired:2 * paired]].set(-surplus)
    live_count = OUT_SLOTS + offsets
    first_serial = jnp.cumsum(live_count) - live_count
    slot_perm = jax.vmap(lambda subkey: jax.random.permutation(subkey, IN_SLOTS))(jax.random.split(subkeys[2], N_DP))
    placed = jnp.argsort(slot_perm, axis=1).astype(jnp.int32)
    is_live = placed < live_count[:, None]
    serial = first_serial[:, None] + placed
    dest_perm = jax.random.permutation(subkeys[3], N_DP).astype(jnp.int32)
    destination = dest_perm[serial // capacity % N_DP]
    arrival = serial // (N_DP * capacity) * capacity + serial % capacity
    land_perm = jax.vmap(lambda subkey: jax.random.permutation(subkey, OUT_SLOTS))(jax.random.split(subkeys[4], N_DP)).astype(jnp.int32)
    landing = land_perm[destination, jnp.clip(arrival, 0, OUT_SLOTS - 1)]
    heights = jax.random.randint(subkeys[5], (N_DP, IN_SLOTS), 8, 65)
    widths = jax.random.randint(subkeys[6], (N_DP, IN_SLOTS), 8, 65)
    partial_value = (heights * widths - 1) % BLK + 1
    complete = jax.random.randint(subkeys[7], (N_DP, IN_SLOTS), 0, 5) < 3
    filled = jnp.where(is_live, jnp.where(complete, BLK, partial_value), 0)
    targets = jnp.where(is_live, destination, -1)
    slots = jnp.where(is_live, landing, -1)
    return jnp.stack([filled, targets, slots]).astype(jnp.int32)


def layout(key):
    columns = jax.vmap(column_layout)(jax.random.split(jax.random.fold_in(key, 11), N_MP))
    return jnp.transpose(columns, (1, 2, 0, 3)).reshape(3, -1)


def draw_fill(key, part):
    return layout(key)[0]


def draw_target(key, part):
    return layout(key)[1]


def draw_target_slot(key, part):
    return layout(key)[2]


def block_scale(key, shape, cuts, least, top_value):
    gain = 1.0
    for dim, shards_of in cuts:
        draws = jax.random.uniform(jax.random.fold_in(jax.random.fold_in(key, 6), dim), (shards_of,), jnp.float32, least / len(cuts), top_value / len(cuts))
        gain = gain * jnp.repeat(jnp.exp(draws), shape[dim] // shards_of).reshape((-1,) + (1,) * (len(shape) - 1 - dim))
    return gain


def gaussian(own_key, dims, deviation, most, shards=(), kind=jnp.bfloat16):
    factor_of = block_scale(own_key, dims, shards, -0.22, 0.18) if shards else 1.0
    entries = jax.random.normal(own_key, dims, jnp.float32) * deviation * factor_of
    return jnp.minimum(jnp.maximum(entries, -most), most).astype(kind)


def setup_inputs(seed: int = 0) -> dict:
    key_list = jax.random.split(jax.random.key(seed), 7)
    latents = gaussian(key_list[0], (NIN * BLK, D), 1.0, 6.0, ((0, 32),))
    proj_weight = gaussian(key_list[1], (BITS, D), D ** -0.5, 0.375)
    proj_bias = gaussian(key_list[2], (BITS,), 0.6, 2.5, (), jnp.float32)
    fill = draw_fill(jax.random.fold_in(key_list[6], 71), 0)
    target = draw_target(jax.random.fold_in(key_list[6], 71), 0)
    target_slot = draw_target_slot(jax.random.fold_in(key_list[6], 71), 0)
    return dict(latents=latents, proj_weight=proj_weight, proj_bias=proj_bias, fill=fill, target=target, target_slot=target_slot)


sharpness = 2.0

def reference(latents, proj_weight, proj_bias, fill, target, target_slot):
    blocks = fill.shape[0]
    token_mask = (jnp.arange(BLK)[None, :] < fill[:, None]).astype(jnp.float32).reshape(-1, 1)
    logits = jnp.dot(latents, proj_weight.T, preferred_element_type=jnp.float32) + proj_bias[None, :]
    scaled = sharpness * logits
    probability = jax.nn.sigmoid(scaled)
    entropy = jax.nn.softplus(scaled) - probability * scaled
    token_count = jnp.sum(fill).astype(jnp.float32)
    marginal = lax.optimization_barrier(jnp.sum(probability * token_mask, axis=0)) / token_count
    entropy_sum = jnp.sum(entropy * token_mask)
    codebook = -jnp.sum(marginal * jnp.log(marginal) + (1.0 - marginal) * jnp.log(1.0 - marginal))
    entropy_loss = entropy_sum / token_count - codebook
    log_odds = jnp.log(1.0 - marginal) - jnp.log(marginal)
    variance = probability * (1.0 - probability) * token_mask
    first_term = -2.0 * scaled * variance
    second_term = 2.0 * variance
    cotangent = (first_term - second_term * log_odds[None, :]).astype(jnp.bfloat16)
    first_rounded = first_term.astype(jnp.bfloat16)
    second_rounded = second_term.astype(jnp.bfloat16)
    contract = (((0,), (0,)), ((), ()))
    first_weight = lax.dot_general(first_rounded, latents, contract, preferred_element_type=jnp.float32)
    second_weight = lax.dot_general(second_rounded, latents, contract, preferred_element_type=jnp.float32)
    weight_grad = (first_weight - second_weight * log_odds[:, None]) / jnp.sqrt(token_count)
    groups = N_DP * N_MP
    grads = lax.map(lambda portion: jnp.dot(portion, proj_weight, preferred_element_type=jnp.float32).astype(jnp.bfloat16), cotangent.reshape(groups, -1, BITS))
    source_block = jnp.arange(blocks).astype(jnp.int32)
    source_mp = source_block // IN_SLOTS % N_MP
    total_out = N_DP * N_MP * OUT_SLOTS
    landing = jnp.where(target >= 0, (target * N_MP + source_mp) * OUT_SLOTS + target_slot, total_out).astype(jnp.int32)
    placed = jnp.zeros((total_out, BLK, D), jnp.bfloat16).at[landing].set(grads.reshape(blocks, BLK, D), mode='drop')
    return (placed.reshape(-1, D), weight_grad, entropy_loss)
```

```python
import functools

import jax
import jax.numpy as jnp
from jax import lax
from jax.experimental import pallas as pl
from jax.experimental.pallas import tpu as pltpu
from jax.sharding import PartitionSpec as P

BLK = 128
OUT_SLOTS = 32
LANES = 128
F32 = jnp.float32
BF16 = jnp.bfloat16
MESH = pl.DeviceIdType.MESH

sharpness = 2.0


def routing(target, target_slot, n_dp, n_mp, in_slots, capacity, own_dp, own_mp):
    shape = (n_dp, n_mp, in_slots)
    col_target = lax.dynamic_index_in_dim(target.reshape(shape), own_mp, 1, keepdims=False)
    col_slot = lax.dynamic_index_in_dim(target_slot.reshape(shape), own_mp, 1, keepdims=False)
    own_target = lax.dynamic_index_in_dim(col_target, own_dp, 0, keepdims=False)
    slots = jnp.arange(in_slots, dtype=jnp.int32)
    earlier = slots[:, None] < slots[None, :]
    own_rank = jnp.sum(((own_target[:, None] == own_target[None, :]) & earlier).astype(jnp.int32), axis=0)
    position = jnp.where(own_target >= 0, own_target * capacity + own_rank, -1)
    sends = jnp.arange(n_dp * capacity, dtype=jnp.int32)
    chosen = jnp.sum(jnp.where(position[None, :] == sends[:, None], slots[None, :], 0), axis=1)
    mine = col_target == own_dp
    rank = jnp.sum((mine[:, :, None] & earlier[None]).astype(jnp.int32), axis=1)
    arrive = jnp.arange(n_dp, dtype=jnp.int32)[:, None] * capacity + rank
    outs = jnp.arange(OUT_SLOTS, dtype=jnp.int32)[:, None, None]
    order = jnp.sum(jnp.where(mine[None] & (col_slot[None] == outs), arrive[None], 0), axis=(1, 2))
    return chosen, order


def wait_bytes(ref, sem):
    pltpu.make_async_copy(ref, ref, sem).wait()


def to_column(row, rows):
    a = lax.broadcasted_iota(jnp.int32, (rows, LANES), 0)
    b = lax.broadcasted_iota(jnp.int32, (rows, LANES), 1)
    return jnp.sum(jnp.where(a == b, jnp.broadcast_to(row, (rows, LANES)), 0.0), axis=1, keepdims=True)


def to_row(column, rows):
    a = lax.broadcasted_iota(jnp.int32, (rows, LANES), 0)
    b = lax.broadcasted_iota(jnp.int32, (rows, LANES), 1)
    return jnp.sum(jnp.where(a == b, jnp.broadcast_to(column, (rows, LANES)), 0.0), axis=0, keepdims=True)


def exchange_kernel(
    n_dp, n_mp, bits, capacity, chunk_slots,
    fill_ref, chosen_ref, count_ref, x_hbm, w_ref, bias_ref,
    land_ref, wg_ref, loss_ref,
    xbuf, first_ref, second_ref, rounded_ref, stat_own, stat_all, send_buf, wg_own, wg_parts, wg_row, wg_all,
    x_sem, stat_send, stat_recv, cot_send, cot_recv, cot_local, part_send, part_recv, row_send, row_recv,
):
    n_dev = n_dp * n_mp
    rows = w_ref.shape[0]
    width = w_ref.shape[1]
    chunk = chunk_slots * BLK
    chunks = xbuf.shape[0] // chunk
    own_dp = lax.axis_index("dp")
    own_mp = lax.axis_index("mp")
    own = own_dp * n_mp + own_mp

    def device(i):
        return {"dp": lax.div(i, n_mp), "mp": lax.rem(i, n_mp)}

    def x_copy(c):
        part = pl.ds(c * chunk, chunk)
        return pltpu.make_async_copy(x_hbm.at[part], xbuf.at[part], x_sem.at[c])

    for c in range(chunks):
        x_copy(c).start()

    barrier = pltpu.get_barrier_semaphore()

    @pl.loop(1, n_dev)
    def _(off):
        pl.semaphore_signal(barrier, inc=1, device_id=device(lax.rem(own + off, n_dev)), device_id_type=MESH)

    bias = bias_ref[...]
    w = w_ref[...]
    live_row = (lax.broadcasted_iota(jnp.int32, (rows, 1), 0) < bits).astype(F32)
    lane = lax.broadcasted_iota(jnp.int32, (1, BLK), 1)

    def statistics(c, carry):
        bit_acc, ent_acc = carry
        x_copy(c).wait()
        x = xbuf[pl.ds(pl.multiple_of(c * chunk, chunk), chunk), :]
        logits = lax.dot_general(w, x, (((1,), (1,)), ((), ())), preferred_element_type=F32) + bias
        scaled = sharpness * logits
        mask = jnp.concatenate(
            [(lane < fill_ref[c * chunk_slots + i]).astype(F32) for i in range(chunk_slots)], axis=1
        )
        size = jnp.abs(scaled)
        e = jnp.exp(-size)
        r = 1.0 / (1.0 + e)
        er = e * r
        prob = jnp.where(scaled >= 0, r, er) * mask
        ent = (jnp.log1p(e) + size * er) * mask
        second = 2.0 * (er * r * mask)
        first = -(scaled * second)
        rounded_ref[c] = jnp.concatenate([first, second], axis=0).astype(BF16)
        for i in range(chunk_slots):
            cols = slice(i * BLK, (i + 1) * BLK)
            first_ref[c * chunk_slots + i] = first[:, cols]
            second_ref[c * chunk_slots + i] = second[:, cols]
            bit_acc = bit_acc + prob[:, cols]
            ent_acc = ent_acc + ent[:, cols]
        return bit_acc, ent_acc

    zero = jnp.zeros((rows, BLK), F32)
    bit_acc, ent_acc = lax.fori_loop(0, chunks, statistics, (zero, zero))
    bit_row = to_row(jnp.sum(bit_acc, axis=1, keepdims=True) * live_row, rows)
    ent_sum = jnp.sum(jnp.sum(ent_acc * live_row, axis=1, keepdims=True), axis=0, keepdims=True)
    lanes = lax.broadcasted_iota(jnp.int32, (1, LANES), 1)
    stat = jnp.where(lanes == LANES - 1, jnp.broadcast_to(ent_sum, (1, LANES)), bit_row)
    stat_own[...] = stat
    stat_all[own] = stat

    pl.semaphore_wait(barrier, n_dev - 1)

    @pl.loop(1, n_dev)
    def _(off):
        pltpu.make_async_remote_copy(
            src_ref=stat_own, dst_ref=stat_all.at[own], send_sem=stat_send, recv_sem=stat_recv,
            device_id=device(lax.rem(own + off, n_dev)), device_id_type=MESH,
        ).start()

    def products(c, acc):
        x = xbuf[pl.ds(pl.multiple_of(c * chunk, chunk), chunk), :]
        return acc + jnp.dot(rounded_ref[c], x, preferred_element_type=F32)

    both = lax.fori_loop(0, chunks, products, jnp.zeros((2 * rows, width), F32))

    wait_bytes(stat_all.at[pl.ds(0, n_dev - 1)], stat_recv)
    total = jnp.sum(stat_all[...], axis=0)
    count = count_ref[0]
    column = to_column(total, rows)
    marginal_c = column / count
    log_odds = jnp.log(1.0 - marginal_c) - jnp.log(marginal_c)
    log_odds = jnp.where(live_row > 0, log_odds, 0.0)

    part = both[:rows] - both[rows:] * log_odds
    for b in range(bits):
        wg_own[b] = part[b:b + 1]

    wg_parts[own] = wg_own[jnp.minimum(own, bits - 1)]

    @pl.loop(0, bits)
    def _(b):
        @pl.when(b != own)
        def _():
            pltpu.make_async_remote_copy(
                src_ref=wg_own.at[b], dst_ref=wg_parts.at[own], send_sem=part_send, recv_sem=part_recv,
                device_id=device(b), device_id_type=MESH,
            ).start()

    @pl.loop(1, n_dp + 1)
    def _(off):
        peer = lax.rem(own_dp + off, n_dp)
        blocks = []
        for k in range(capacity):
            slot = chosen_ref[peer * capacity + k]
            blocks.append((first_ref[slot] - second_ref[slot] * log_odds)[:bits])
        send_buf[peer] = jnp.concatenate(blocks, axis=0).astype(BF16)

        @pl.when(off < n_dp)
        def _():
            pltpu.make_async_remote_copy(
                src_ref=send_buf.at[peer], dst_ref=land_ref.at[own_dp], send_sem=cot_send, recv_sem=cot_recv,
                device_id={"dp": peer, "mp": own_mp}, device_id_type=MESH,
            ).start()

    keep = pltpu.make_async_copy(send_buf.at[own_dp], land_ref.at[own_dp], cot_local)
    keep.start()

    marginal = total / count
    inside = lanes < bits
    safe = jnp.where(inside, marginal, 0.5)
    plain = safe * jnp.log(safe) + (1.0 - safe) * jnp.log(1.0 - safe)
    neg_codebook = jnp.sum(jnp.where(inside, plain, 0.0), axis=1, keepdims=True)
    ent_all = jnp.sum(jnp.where(lanes == LANES - 1, total, 0.0), axis=1, keepdims=True)
    loss_ref[...] = jnp.broadcast_to(ent_all / count + neg_codebook, (1, LANES))

    @pl.when(own < bits)
    def _():
        wait_bytes(wg_parts.at[pl.ds(0, n_dev - 1)], part_recv)
        row = jnp.sum(wg_parts[...], axis=0) / jnp.sqrt(jnp.full((1, width), count, F32))
        wg_row[...] = row
        wg_all[own] = row

        @pl.loop(1, n_dev)
        def _(off):
            pltpu.make_async_remote_copy(
                src_ref=wg_row, dst_ref=wg_all.at[own], send_sem=row_send, recv_sem=row_recv,
                device_id=device(lax.rem(own + off, n_dev)), device_id_type=MESH,
            ).start()

        wait_bytes(wg_all.at[pl.ds(0, bits - 1)], row_recv)
        wait_bytes(wg_own.at[pl.ds(0, bits - 1)], part_send)
        wait_bytes(wg_parts.at[pl.ds(0, n_dev - 1)], row_send)

    @pl.when(own >= bits)
    def _():
        wait_bytes(wg_all.at[pl.ds(0, bits)], row_recv)
        wait_bytes(wg_own.at[pl.ds(0, bits)], part_send)

    wg_ref[...] = wg_all[...]
    wait_bytes(stat_all.at[pl.ds(0, n_dev - 1)], stat_send)
    keep.wait()
    wait_bytes(send_buf.at[pl.ds(0, n_dp - 1)], cot_send)
    wait_bytes(land_ref.at[pl.ds(0, n_dp - 1)], cot_recv)


def finish_kernel(n_dp, bits, capacity, step_blocks, order_ref, land_ref, w_ref, wg_ref, out_ref, wg_out, blocks):
    @pl.when(pl.program_id(0) == 0)
    def _():
        for src in range(n_dp):
            rows = land_ref[src].astype(F32)
            for k in range(capacity):
                blocks[src * capacity + k] = rows[k * bits:(k + 1) * bits]
        for b in range(bits):
            wg_out[b:b + 1, :] = wg_ref[b]

    w = w_ref[...]
    for i in range(step_blocks):
        cot = blocks[order_ref[pl.program_id(0) * step_blocks + i]].astype(BF16)
        out_ref[i * BLK:(i + 1) * BLK, :] = lax.dot_general(
            cot, w, (((0,), (0,)), ((), ())), preferred_element_type=F32
        ).astype(BF16)


def local(latents, proj_weight, proj_bias, fill, target, target_slot):
    n_dp = lax.axis_size("dp")
    n_mp = lax.axis_size("mp")
    n_dev = n_dp * n_mp
    own_dp = lax.axis_index("dp")
    own_mp = lax.axis_index("mp")
    width = latents.shape[1]
    bits = proj_weight.shape[0]
    in_slots = latents.shape[0] // BLK
    capacity = max(1, 2 * OUT_SLOTS // n_dp)
    rows = -(-bits // 8) * 8
    chunk_slots = 8
    chunks = in_slots // chunk_slots
    chosen, order = routing(target, target_slot, n_dp, n_mp, in_slots, capacity, own_dp, own_mp)
    own_fill = lax.dynamic_slice(fill, ((own_dp * n_mp + own_mp) * in_slots,), (in_slots,))
    count = jnp.sum(fill).astype(F32).reshape(1)
    w_pad = jnp.pad(proj_weight, ((0, rows - bits), (0, 0)))
    bias_pad = jnp.pad(proj_bias, (0, rows - bits)).reshape(rows, 1)
    smem = pl.BlockSpec(memory_space=pltpu.SMEM)
    vmem = pl.BlockSpec(memory_space=pltpu.VMEM)
    hbm = pl.BlockSpec(memory_space=pl.ANY)
    dma = pltpu.SemaphoreType.DMA
    land, wg, loss = pl.pallas_call(
        functools.partial(exchange_kernel, n_dp, n_mp, bits, capacity, chunk_slots),
        out_shape=(
            jax.ShapeDtypeStruct((n_dp, capacity * bits, BLK), BF16),
            jax.ShapeDtypeStruct((bits, 1, width), F32),
            jax.ShapeDtypeStruct((1, LANES), F32),
        ),
        in_specs=[smem, smem, smem, hbm, vmem, vmem],
        out_specs=(hbm, vmem, vmem),
        scratch_shapes=[
            pltpu.VMEM(latents.shape, BF16),
            pltpu.VMEM((in_slots, rows, BLK), F32),
            pltpu.VMEM((in_slots, rows, BLK), F32),
            pltpu.VMEM((chunks, 2 * rows, chunk_slots * BLK), BF16),
            pltpu.VMEM((1, LANES), F32),
            pltpu.VMEM((n_dev, 1, LANES), F32),
            pltpu.VMEM((n_dp, capacity * bits, BLK), BF16),
            pltpu.VMEM((bits, 1, width), F32),
            pltpu.VMEM((n_dev, 1, width), F32),
            pltpu.VMEM((1, width), F32),
            pltpu.VMEM((bits, 1, width), F32),
            dma((chunks,)),
        ] + [dma(())] * 9,
        compiler_params=pltpu.CompilerParams(
            collective_id=0, has_side_effects=True, vmem_limit_bytes=32 * 1024 * 1024
        ),
        name="exchange",
    )(own_fill, chosen, count, latents, w_pad, bias_pad)
    step_blocks = 8
    grad, wg = pl.pallas_call(
        functools.partial(finish_kernel, n_dp, bits, capacity, step_blocks),
        out_shape=(
            jax.ShapeDtypeStruct((OUT_SLOTS * BLK, width), BF16),
            jax.ShapeDtypeStruct((bits, width), F32),
        ),
        grid_spec=pltpu.PrefetchScalarGridSpec(
            num_scalar_prefetch=1,
            grid=(OUT_SLOTS // step_blocks,),
            in_specs=[vmem, vmem, vmem],
            out_specs=(
                pl.BlockSpec((step_blocks * BLK, width), lambda g, order: (g, 0)),
                pl.BlockSpec((bits, width), lambda g, order: (0, 0)),
            ),
            scratch_shapes=[pltpu.VMEM((n_dp * capacity, bits, BLK), F32)],
        ),
        name="finish",
    )(order, land, proj_weight, wg)
    return grad, wg, loss[0, 0]


def solution(mesh):
    placed = (P(("dp", "mp"), None), P(), P(), P(), P(), P())
    return jax.shard_map(
        local,
        mesh=mesh,
        in_specs=placed,
        out_specs=(P(("dp", "mp"), None), P(), P()),
        check_vma=False,
    )
```

```python
import functools

import jax
import jax.numpy as jnp
from jax import lax
from jax.experimental import pallas as pl
from jax.experimental.pallas import tpu as pltpu
from jax.sharding import PartitionSpec as P

BLK = 128
OUT_SLOTS = 32
LANES = 128
F32 = jnp.float32
BF16 = jnp.bfloat16
MESH = pl.DeviceIdType.MESH

sharpness = 2.0


def wait_bytes(ref, sem):
    pltpu.make_async_copy(ref, ref, sem).wait()


def to_column(row, rows):
    shape = (rows, row.shape[1])
    diagonal = lax.broadcasted_iota(jnp.int32, shape, 0) == lax.broadcasted_iota(jnp.int32, shape, 1)
    return jnp.sum(jnp.where(diagonal, jnp.broadcast_to(row, shape), 0.0), axis=1, keepdims=True)


def to_row(column):
    shape = (column.shape[0], LANES)
    diagonal = lax.broadcasted_iota(jnp.int32, shape, 0) == lax.broadcasted_iota(jnp.int32, shape, 1)
    return jnp.sum(jnp.where(diagonal, jnp.broadcast_to(column, shape), 0.0), axis=0, keepdims=True)


def slot_row(ref, index, in_slots):
    per = LANES // in_slots
    line = ref[pl.ds(lax.div(index, per), 1), :].astype(F32)
    which = lax.rem(index, per)
    row = line[:, :in_slots]
    for i in range(1, per):
        row = jnp.where(which == i, line[:, i * in_slots:(i + 1) * in_slots], row)
    return row


def exchange_kernel(
    n_dp, n_mp, bits, capacity, chunk_slots,
    fill_hbm, target_hbm, slot_hbm, x_hbm, w_ref, bias_ref,
    cot_ref, wg_ref, loss_ref,
    xbuf, fill_ref, target_ref, slot_ref, mask_ref, first_ref, second_ref, rounded_ref, stat_own, stat_all,
    send_buf, land, landed, mine_ref, index_vec, chosen_ref, order_ref, wg_own, wg_parts, wg_row, wg_all,
    x_sem, small_sem, index_sem, stat_send, stat_recv, cot_send, cot_recv, part_send, part_recv, row_send, row_recv,
):
    n_dev = n_dp * n_mp
    rows = first_ref.shape[1]
    in_slots = first_ref.shape[0]
    width = w_ref.shape[1]
    out_slots = cot_ref.shape[1] // BLK
    chunk = chunk_slots * BLK
    chunks = xbuf.shape[0] // chunk
    own_dp = lax.axis_index("dp")
    own_mp = lax.axis_index("mp")
    own = own_dp * n_mp + own_mp

    def device(i):
        return {"dp": lax.div(i, n_mp), "mp": lax.rem(i, n_mp)}

    def x_copy(c):
        part = pl.ds(c * chunk, chunk)
        return pltpu.make_async_copy(x_hbm.at[part], xbuf.at[part], x_sem.at[c])

    small = [
        pltpu.make_async_copy(src, dst, small_sem.at[i])
        for i, (src, dst) in enumerate(((fill_hbm, fill_ref), (target_hbm, target_ref), (slot_hbm, slot_ref)))
    ]
    for copy in small:
        copy.start()
    for c in range(chunks):
        x_copy(c).start()

    barrier = pltpu.get_barrier_semaphore()

    @pl.loop(1, n_dev)
    def _(off):
        pl.semaphore_signal(barrier, inc=1, device_id=device(lax.rem(own + off, n_dev)), device_id_type=MESH)

    bias = to_column(bias_ref[...], rows)
    w = w_ref[...]
    w = jnp.concatenate([w.astype(F32), jnp.zeros((rows - bits, width), F32)], axis=0).astype(BF16)
    for copy in small:
        copy.wait()
    fill_col = to_column(slot_row(fill_ref, own, in_slots), in_slots)
    token = lax.broadcasted_iota(jnp.int32, (in_slots, BLK), 1).astype(F32)
    mask_ref[...] = (token < fill_col).astype(F32)
    fills = fill_ref[...].astype(F32)
    count = jnp.sum(jnp.sum(fills, axis=0, keepdims=True), axis=1, keepdims=True)
    live_row = (lax.broadcasted_iota(jnp.int32, (rows, 1), 0) < bits).astype(F32)

    def statistics(c, carry):
        bit_acc, ent_acc = carry
        x_copy(c).wait()
        x = xbuf[pl.ds(pl.multiple_of(c * chunk, chunk), chunk), :]
        logits = lax.dot_general(w, x, (((1,), (1,)), ((), ())), preferred_element_type=F32) + bias
        scaled = sharpness * logits
        mask = jnp.concatenate(
            [mask_ref[pl.ds(c * chunk_slots + i, 1), :] for i in range(chunk_slots)], axis=1
        )
        size = jnp.abs(scaled)
        e = jnp.exp(-size)
        r = 1.0 / (1.0 + e)
        er = e * r
        prob = jnp.where(scaled >= 0, r, er) * mask
        ent = (jnp.log1p(e) + size * er) * mask
        second = 2.0 * (er * r * mask)
        first = -(scaled * second)
        rounded_ref[c] = jnp.concatenate([first, second], axis=0).astype(BF16)
        for i in range(chunk_slots):
            cols = slice(i * BLK, (i + 1) * BLK)
            first_ref[c * chunk_slots + i] = first[:, cols]
            second_ref[c * chunk_slots + i] = second[:, cols]
            bit_acc = bit_acc + prob[:, cols]
            ent_acc = ent_acc + ent[:, cols]
        return bit_acc, ent_acc

    zero = jnp.zeros((rows, BLK), F32)
    bit_acc, ent_acc = lax.fori_loop(0, chunks, statistics, (zero, zero))
    bit_row = to_row(jnp.sum(bit_acc, axis=1, keepdims=True) * live_row)
    ent_sum = jnp.sum(jnp.sum(ent_acc * live_row, axis=1, keepdims=True), axis=0, keepdims=True)
    lanes = lax.broadcasted_iota(jnp.int32, (1, LANES), 1)
    stat = jnp.where(lanes == LANES - 1, jnp.broadcast_to(ent_sum, (1, LANES)), bit_row)
    stat_own[...] = stat
    stat_all[own] = stat

    pl.semaphore_wait(barrier, n_dev - 1)

    @pl.loop(1, n_dev)
    def _(off):
        pltpu.make_async_remote_copy(
            src_ref=stat_own, dst_ref=stat_all.at[own], send_sem=stat_send, recv_sem=stat_recv,
            device_id=device(lax.rem(own + off, n_dev)), device_id_type=MESH,
        ).start()

    target_row = slot_row(target_ref, own, in_slots)
    target_col = to_column(target_row, in_slots)
    before = lax.broadcasted_iota(jnp.int32, (in_slots, in_slots), 1) < lax.broadcasted_iota(
        jnp.int32, (in_slots, in_slots), 0
    )
    rank = jnp.sum(jnp.where((target_col == target_row) & before, 1.0, 0.0), axis=1, keepdims=True)
    position = jnp.where(target_col >= 0.0, target_col * float(capacity) + rank, -1.0)
    send_lane = lax.broadcasted_iota(jnp.int32, (in_slots, LANES), 1).astype(F32)
    send_slot = lax.broadcasted_iota(jnp.int32, (in_slots, LANES), 0).astype(F32)
    chosen = jnp.sum(jnp.where(position == send_lane, send_slot, 0.0), axis=0, keepdims=True)
    index_vec[0] = chosen.astype(jnp.int32)
    choose = pltpu.make_async_copy(index_vec.at[0], chosen_ref, index_sem.at[0])
    choose.start()

    def products(c, acc):
        x = xbuf[pl.ds(pl.multiple_of(c * chunk, chunk), chunk), :]
        return acc + jnp.dot(rounded_ref[c], x, preferred_element_type=F32)

    both = lax.fori_loop(0, chunks, products, jnp.zeros((2 * rows, width), F32))

    wait_bytes(stat_all.at[pl.ds(0, n_dev - 1)], stat_recv)
    total = jnp.sum(stat_all[...], axis=0)
    column = to_column(total, rows)
    marginal_c = column / count
    log_odds = jnp.log(1.0 - marginal_c) - jnp.log(marginal_c)
    log_odds = jnp.where(live_row > 0, log_odds, 0.0)

    choose.wait()
    part = both[:rows] - both[rows:] * log_odds
    for b in range(bits):
        wg_own[b] = part[b:b + 1]

    wg_parts[own] = wg_own[jnp.minimum(own, bits - 1)]

    @pl.loop(0, bits)
    def _(b):
        @pl.when(b != own)
        def _():
            pltpu.make_async_remote_copy(
                src_ref=wg_own.at[b], dst_ref=wg_parts.at[own], send_sem=part_send, recv_sem=part_recv,
                device_id=device(b), device_id_type=MESH,
            ).start()

    @pl.loop(1, n_dp + 1)
    def _(off):
        peer = lax.rem(own_dp + off, n_dp)
        blocks = []
        for k in range(capacity):
            slot = jnp.clip(chosen_ref[0, peer * capacity + k], 0, in_slots - 1)
            blocks.append((first_ref[slot] - second_ref[slot] * log_odds)[:bits])
        packed = jnp.concatenate(blocks, axis=0).astype(BF16)

        @pl.when(off == n_dp)
        def _():
            land[own_dp] = packed

        @pl.when(off < n_dp)
        def _():
            send_buf[peer] = packed
            pltpu.make_async_remote_copy(
                src_ref=send_buf.at[peer], dst_ref=land.at[own_dp], send_sem=cot_send, recv_sem=cot_recv.at[own_dp],
                device_id={"dp": peer, "mp": own_mp}, device_id_type=MESH,
            ).start()

    for d in range(n_dp):
        mine_ref[d:d + 1, :] = jnp.where(slot_row(target_ref, d * n_mp + own_mp, in_slots) == own_dp.astype(F32), 1.0, 0.0)
    mine = mine_ref[...]
    later = lax.broadcasted_iota(jnp.int32, (in_slots, in_slots), 0) < lax.broadcasted_iota(
        jnp.int32, (in_slots, in_slots), 1
    )
    ranks = jnp.dot(mine.astype(BF16), later.astype(F32).astype(BF16), preferred_element_type=F32)
    out_index = lax.broadcasted_iota(jnp.int32, (out_slots, in_slots), 0).astype(F32)
    gathered = jnp.zeros((out_slots, in_slots), F32)
    for d in range(n_dp):
        slots = slot_row(slot_ref, d * n_mp + own_mp, in_slots)
        arrive = float(d * capacity) + ranks[d:d + 1]
        gathered = gathered + jnp.where((out_index == slots) & (mine[d:d + 1] > 0.0), arrive, 0.0)
    order = to_row(jnp.sum(gathered, axis=1, keepdims=True))
    index_vec[1] = order.astype(jnp.int32)
    ordering = pltpu.make_async_copy(index_vec.at[1], order_ref, index_sem.at[1])
    ordering.start()

    marginal = total / count
    inside = lanes < bits
    safe = jnp.where(inside, marginal, 0.5)
    plain = safe * jnp.log(safe) + (1.0 - safe) * jnp.log(1.0 - safe)
    neg_codebook = jnp.sum(jnp.where(inside, plain, 0.0), axis=1, keepdims=True)
    ent_all = jnp.sum(jnp.where(lanes == LANES - 1, total, 0.0), axis=1, keepdims=True)
    loss_ref[...] = jnp.broadcast_to(ent_all / count + neg_codebook, (1, LANES))

    @pl.when(own < bits)
    def _():
        wait_bytes(wg_parts.at[pl.ds(0, n_dev - 1)], part_recv)
        row = jnp.sum(wg_parts[...], axis=0) / jnp.sqrt(count)
        wg_row[...] = row
        wg_all[own] = row

        @pl.loop(1, n_dev)
        def _(off):
            pltpu.make_async_remote_copy(
                src_ref=wg_row, dst_ref=wg_all.at[own], send_sem=row_send, recv_sem=row_recv,
                device_id=device(lax.rem(own + off, n_dev)), device_id_type=MESH,
            ).start()

        wait_bytes(wg_all.at[pl.ds(0, bits - 1)], row_recv)
        wait_bytes(wg_own.at[pl.ds(0, bits - 1)], part_send)
        wait_bytes(wg_parts.at[pl.ds(0, n_dev - 1)], row_send)

    @pl.when(own >= bits)
    def _():
        wait_bytes(wg_all.at[pl.ds(0, bits)], row_recv)
        wait_bytes(wg_own.at[pl.ds(0, bits)], part_send)

    wg_ref[...] = wg_all[...]
    wait_bytes(stat_all.at[pl.ds(0, n_dev - 1)], stat_send)
    ordering.wait()

    @pl.loop(0, n_dp)
    def _(off):
        src = lax.rem(own_dp + n_dp - off, n_dp)

        @pl.when(off > 0)
        def _():
            wait_bytes(land.at[src], cot_recv.at[src])

        arrived = land[src].astype(F32)
        for k in range(capacity):
            landed[src * capacity + k] = arrived[k * bits:(k + 1) * bits]

    for k in range(out_slots):
        cot_ref[:, k * BLK:(k + 1) * BLK] = landed[jnp.clip(order_ref[0, k], 0, n_dp * capacity - 1)].astype(BF16)
    wait_bytes(send_buf.at[pl.ds(0, n_dp - 1)], cot_send)


def finish_kernel(cot_ref, w_ref, wg_ref, out_ref, wg_out):
    @pl.when(pl.program_id(0) == 0)
    def _():
        for b in range(wg_ref.shape[0]):
            wg_out[b:b + 1, :] = wg_ref[b]

    out_ref[...] = lax.dot_general(
        cot_ref[...], w_ref[...], (((0,), (0,)), ((), ())), preferred_element_type=F32
    ).astype(BF16)


def local(latents, proj_weight, proj_bias, fill, target, target_slot):
    n_dp = lax.axis_size("dp")
    n_mp = lax.axis_size("mp")
    n_dev = n_dp * n_mp
    width = latents.shape[1]
    bits = proj_weight.shape[0]
    in_slots = latents.shape[0] // BLK
    capacity = max(1, 2 * OUT_SLOTS // n_dp)
    rows = -(-bits // 8) * 8
    chunk_slots = 8
    chunks = in_slots // chunk_slots
    sends = n_dp * capacity
    table = (fill.shape[0] // LANES, LANES)
    smem = pltpu.SMEM
    vmem = pl.BlockSpec(memory_space=pltpu.VMEM)
    hbm = pl.BlockSpec(memory_space=pltpu.HBM)
    dma = pltpu.SemaphoreType.DMA
    cot, wg, loss = pl.pallas_call(
        functools.partial(exchange_kernel, n_dp, n_mp, bits, capacity, chunk_slots),
        out_shape=(
            jax.ShapeDtypeStruct((bits, OUT_SLOTS * BLK), BF16),
            jax.ShapeDtypeStruct((bits, 1, width), F32),
            jax.ShapeDtypeStruct((1, LANES), F32),
        ),
        in_specs=[hbm, hbm, hbm, hbm, vmem, vmem],
        out_specs=(vmem, vmem, vmem),
        scratch_shapes=[
            pltpu.VMEM(latents.shape, BF16),
            pltpu.VMEM(table, jnp.int32),
            pltpu.VMEM(table, jnp.int32),
            pltpu.VMEM(table, jnp.int32),
            pltpu.VMEM((in_slots, BLK), F32),
            pltpu.VMEM((in_slots, rows, BLK), F32),
            pltpu.VMEM((in_slots, rows, BLK), F32),
            pltpu.VMEM((chunks, 2 * rows, chunk_slots * BLK), BF16),
            pltpu.VMEM((1, LANES), F32),
            pltpu.VMEM((n_dev, 1, LANES), F32),
            pltpu.VMEM((n_dp, capacity * bits, BLK), BF16),
            pltpu.VMEM((n_dp, capacity * bits, BLK), BF16),
            pltpu.VMEM((sends, bits, BLK), F32),
            pltpu.VMEM((n_dp, in_slots), F32),
            pltpu.VMEM((2, 1, LANES), jnp.int32),
            smem((1, LANES), jnp.int32),
            smem((1, LANES), jnp.int32),
            pltpu.VMEM((bits, 1, width), F32),
            pltpu.VMEM((n_dev, 1, width), F32),
            pltpu.VMEM((1, width), F32),
            pltpu.VMEM((bits, 1, width), F32),
            dma((chunks,)), dma((3,)), dma((2,)), dma(()), dma(()), dma(()), dma((n_dp,)),
            dma(()), dma(()), dma(()), dma(()),
        ],
        compiler_params=pltpu.CompilerParams(
            collective_id=0, has_side_effects=True, vmem_limit_bytes=67043328
        ),
        name="exchange",
    )(fill.reshape(table), target.reshape(table), target_slot.reshape(table), latents, proj_weight,
      proj_bias.reshape(1, bits))
    step = 1024
    grad, wg = pl.pallas_call(
        finish_kernel,
        out_shape=(
            jax.ShapeDtypeStruct((OUT_SLOTS * BLK, width), BF16),
            jax.ShapeDtypeStruct((bits, width), F32),
        ),
        grid=(OUT_SLOTS * BLK // step,),
        in_specs=[
            pl.BlockSpec((bits, step), lambda g: (0, g)),
            pl.BlockSpec((bits, width), lambda g: (0, 0)),
            pl.BlockSpec((bits, 1, width), lambda g: (0, 0, 0)),
        ],
        out_specs=(
            pl.BlockSpec((step, width), lambda g: (g, 0)),
            pl.BlockSpec((bits, width), lambda g: (0, 0)),
        ),
        name="finish",
    )(cot, proj_weight, wg)
    return grad, wg, loss[0, 0]


def solution(mesh):
    placed = (P(("dp", "mp"), None), P(), P(), P(), P(), P())
    return jax.shard_map(
        local,
        mesh=mesh,
        in_specs=placed,
        out_specs=(P(("dp", "mp"), None), P(), P()),
        check_vma=False,
    )
```

```python
import functools

import jax
import jax.numpy as jnp
from jax import lax
from jax.experimental import pallas as pl
from jax.experimental.pallas import tpu as pltpu
from jax.sharding import PartitionSpec as P

BLK = 128
OUT_SLOTS = 32
LANES = 128
F32 = jnp.float32
BF16 = jnp.bfloat16
MESH = pl.DeviceIdType.MESH

sharpness = 2.0


def wait_bytes(ref, sem):
    pltpu.make_async_copy(ref, ref, sem).wait()


def to_column(row, rows):
    shape = (rows, row.shape[1])
    diagonal = lax.broadcasted_iota(jnp.int32, shape, 0) == lax.broadcasted_iota(jnp.int32, shape, 1)
    return jnp.sum(jnp.where(diagonal, jnp.broadcast_to(row, shape), 0.0), axis=1, keepdims=True)


def to_row(column):
    shape = (column.shape[0], LANES)
    diagonal = lax.broadcasted_iota(jnp.int32, shape, 0) == lax.broadcasted_iota(jnp.int32, shape, 1)
    return jnp.sum(jnp.where(diagonal, jnp.broadcast_to(column, shape), 0.0), axis=0, keepdims=True)


def slot_row(ref, index, in_slots):
    per = LANES // in_slots
    line = ref[pl.ds(lax.div(index, per), 1), :].astype(F32)
    which = lax.rem(index, per)
    row = line[:, :in_slots]
    for i in range(1, per):
        row = jnp.where(which == i, line[:, i * in_slots:(i + 1) * in_slots], row)
    return row


def exchange_kernel(
    n_dp, n_mp, capacity, chunk_slots,
    fill_hbm, target_hbm, slot_hbm, x_hbm, w_ref, bias_ref,
    cot_ref, wg_ref, loss_ref,
    xbuf, fill_ref, target_ref, slot_ref, mask_ref, out_mask, scaled_ref, stat_own, stat_all,
    send_buf, land, mine_ref, index_vec, chosen_ref, order_ref, wg_own, wg_parts, wg_row, wg_all,
    x_sem, small_sem, index_sem, stat_send, stat_recv, cot_send, cot_recv, part_send, part_recv, row_send, row_recv,
):
    n_dev = n_dp * n_mp
    in_slots, rows, _ = scaled_ref.shape
    bits, width = w_ref.shape
    out_slots = cot_ref.shape[0]
    chunk = chunk_slots * BLK
    chunks = xbuf.shape[0] // chunk
    own_dp = lax.axis_index("dp")
    own_mp = lax.axis_index("mp")
    own = own_dp * n_mp + own_mp

    def device(i):
        return {"dp": lax.div(i, n_mp), "mp": lax.rem(i, n_mp)}

    def x_copy(c):
        part = pl.ds(c * chunk, chunk)
        return pltpu.make_async_copy(x_hbm.at[part], xbuf.at[part], x_sem.at[c])

    small = [
        pltpu.make_async_copy(src, dst, small_sem.at[i])
        for i, (src, dst) in enumerate(((fill_hbm, fill_ref), (target_hbm, target_ref), (slot_hbm, slot_ref)))
    ]
    for copy in small:
        copy.start()
    for c in range(chunks):
        x_copy(c).start()

    barrier = pltpu.get_barrier_semaphore()

    @pl.loop(1, n_dev)
    def _(off):
        pl.semaphore_signal(barrier, inc=1, device_id=device(lax.rem(own + off, n_dev)), device_id_type=MESH)

    bias = to_column(bias_ref[...], rows)
    w = w_ref[...]
    w = jnp.concatenate([w.astype(F32), jnp.zeros((rows - bits, width), F32)], axis=0).astype(BF16)
    live_row = (lax.broadcasted_iota(jnp.int32, (rows, 1), 0) < bits).astype(F32)
    lanes = lax.broadcasted_iota(jnp.int32, (1, LANES), 1)
    for copy in small:
        copy.wait()

    target_row = slot_row(target_ref, own, in_slots)
    target_col = to_column(target_row, in_slots)
    before = lax.broadcasted_iota(jnp.int32, (in_slots, in_slots), 1) < lax.broadcasted_iota(
        jnp.int32, (in_slots, in_slots), 0
    )
    rank = jnp.sum(jnp.where((target_col == target_row) & before, 1.0, 0.0), axis=1, keepdims=True)
    position = jnp.where(target_col >= 0.0, target_col * float(capacity) + rank, -1.0)
    send_lane = lax.broadcasted_iota(jnp.int32, (in_slots, LANES), 1).astype(F32)
    send_slot = lax.broadcasted_iota(jnp.int32, (in_slots, LANES), 0).astype(F32)
    chosen = jnp.sum(jnp.where(position == send_lane, send_slot, 0.0), axis=0, keepdims=True)
    index_vec[0] = chosen.astype(jnp.int32)
    choose = pltpu.make_async_copy(index_vec.at[0], chosen_ref, index_sem.at[0])
    choose.start()

    fill_col = to_column(slot_row(fill_ref, own, in_slots), in_slots)
    token = lax.broadcasted_iota(jnp.int32, (in_slots, BLK), 1).astype(F32)
    mask_ref[...] = (token < fill_col).astype(F32)
    fills = fill_ref[...].astype(F32)
    count = jnp.sum(jnp.sum(fills, axis=0, keepdims=True), axis=1, keepdims=True)

    @pl.loop(0, chunks)
    def _(c):
        x_copy(c).wait()
        x = xbuf[pl.ds(pl.multiple_of(c * chunk, chunk), chunk), :]
        logits = lax.dot_general(w, x, (((1,), (1,)), ((), ())), preferred_element_type=F32) + bias
        scaled = sharpness * logits
        for i in range(chunk_slots):
            scaled_ref[c * chunk_slots + i] = scaled[:, i * BLK:(i + 1) * BLK]

    choose.wait()
    pl.semaphore_wait(barrier, n_dev - 1)

    @pl.loop(1, n_dp + 1)
    def _(off):
        peer = lax.rem(own_dp + off, n_dp)

        def pack(ref):
            for k in range(capacity):
                slot = jnp.clip(chosen_ref[0, peer * capacity + k], 0, in_slots - 1)
                ref[peer, k * bits:(k + 1) * bits, :] = scaled_ref[slot][:bits]

        @pl.when(off == n_dp)
        def _():
            pack(land)

        @pl.when(off < n_dp)
        def _():
            pack(send_buf)
            pltpu.make_async_remote_copy(
                src_ref=send_buf.at[peer], dst_ref=land.at[own_dp], send_sem=cot_send, recv_sem=cot_recv,
                device_id={"dp": peer, "mp": own_mp}, device_id_type=MESH,
            ).start()

    def statistics(c, carry):
        bit_acc, ent_acc, both = carry
        x = xbuf[pl.ds(pl.multiple_of(c * chunk, chunk), chunk), :]
        scaled = jnp.concatenate([scaled_ref[c * chunk_slots + i] for i in range(chunk_slots)], axis=1)
        mask = jnp.concatenate(
            [mask_ref[pl.ds(c * chunk_slots + i, 1), :] for i in range(chunk_slots)], axis=1
        )
        size = jnp.abs(scaled)
        e = jnp.exp(-size)
        u = 1.0 + e
        r = 1.0 / u
        er = e * r
        prob = jnp.where(scaled >= 0, r, er) * mask
        ent = (jnp.log(u) + (e - (u - 1.0)) * r + size * er) * mask
        second = 2.0 * (er * r * mask)
        first = -(scaled * second)
        rounded = jnp.concatenate([first, second], axis=0).astype(BF16)
        both = both + jnp.dot(rounded, x, preferred_element_type=F32)
        for i in range(chunk_slots):
            cols = slice(i * BLK, (i + 1) * BLK)
            bit_acc = bit_acc + prob[:, cols]
            ent_acc = ent_acc + ent[:, cols]
        return bit_acc, ent_acc, both

    zero = jnp.zeros((rows, BLK), F32)
    bit_acc, ent_acc, both = lax.fori_loop(
        0, chunks, statistics, (zero, zero, jnp.zeros((2 * rows, width), F32))
    )
    bit_row = to_row(jnp.sum(bit_acc, axis=1, keepdims=True) * live_row)
    ent_sum = jnp.sum(jnp.sum(ent_acc * live_row, axis=1, keepdims=True), axis=0, keepdims=True)
    stat = jnp.where(lanes == LANES - 1, jnp.broadcast_to(ent_sum, (1, LANES)), bit_row)
    stat_own[...] = stat
    stat_all[own] = stat
    for b in range(bits):
        wg_own[b, 0:1, :] = both[b:b + 1]
        wg_own[b, 1:2, :] = both[rows + b:rows + b + 1]
    wg_parts[own] = wg_own[jnp.minimum(own, bits - 1)]

    @pl.loop(1, n_dev)
    def _(off):
        pltpu.make_async_remote_copy(
            src_ref=stat_own, dst_ref=stat_all.at[own], send_sem=stat_send, recv_sem=stat_recv,
            device_id=device(lax.rem(own + off, n_dev)), device_id_type=MESH,
        ).start()

    @pl.loop(0, bits)
    def _(b):
        @pl.when(b != own)
        def _():
            pltpu.make_async_remote_copy(
                src_ref=wg_own.at[b], dst_ref=wg_parts.at[own], send_sem=part_send, recv_sem=part_recv,
                device_id=device(b), device_id_type=MESH,
            ).start()

    for d in range(n_dp):
        mine_ref[d:d + 1, :] = jnp.where(slot_row(target_ref, d * n_mp + own_mp, in_slots) == own_dp.astype(F32), 1.0, 0.0)
    mine = mine_ref[...]
    later = lax.broadcasted_iota(jnp.int32, (in_slots, in_slots), 0) < lax.broadcasted_iota(
        jnp.int32, (in_slots, in_slots), 1
    )
    ranks = jnp.dot(mine.astype(BF16), later.astype(F32).astype(BF16), preferred_element_type=F32)
    out_index = lax.broadcasted_iota(jnp.int32, (out_slots, in_slots), 0).astype(F32)
    gathered = jnp.zeros((out_slots, in_slots), F32)
    out_fill = jnp.zeros((out_slots, in_slots), F32)
    for d in range(n_dp):
        taken = (out_index == slot_row(slot_ref, d * n_mp + own_mp, in_slots)) & (mine[d:d + 1] > 0.0)
        gathered = gathered + jnp.where(taken, float(d * capacity) + ranks[d:d + 1], 0.0)
        out_fill = out_fill + jnp.where(taken, slot_row(fill_ref, d * n_mp + own_mp, in_slots), 0.0)
    index_vec[1] = to_row(jnp.sum(gathered, axis=1, keepdims=True)).astype(jnp.int32)
    ordering = pltpu.make_async_copy(index_vec.at[1], order_ref, index_sem.at[1])
    ordering.start()
    out_token = lax.broadcasted_iota(jnp.int32, (out_slots, BLK), 1).astype(F32)
    out_mask[...] = (out_token < jnp.sum(out_fill, axis=1, keepdims=True)).astype(F32)

    wait_bytes(stat_all.at[pl.ds(0, n_dev - 1)], stat_recv)
    total = jnp.sum(stat_all[...], axis=0)
    marginal_c = to_column(total, rows) / count
    log_odds = jnp.log(1.0 - marginal_c) - jnp.log(marginal_c)
    log_odds = jnp.where(live_row > 0, log_odds, 0.0)

    @pl.when(own < bits)
    def _():
        row_index = lax.broadcasted_iota(jnp.int32, (rows, 1), 0)
        own_odds = jnp.sum(jnp.where(row_index == own, log_odds, 0.0), axis=0, keepdims=True)
        wait_bytes(wg_parts.at[pl.ds(0, n_dev - 1)], part_recv)
        parts = jnp.sum(wg_parts[...], axis=0)
        row = (parts[0:1] - parts[1:2] * own_odds) / jnp.sqrt(count)
        wg_row[...] = row
        wg_all[own] = row

        @pl.loop(1, n_dev)
        def _(off):
            pltpu.make_async_remote_copy(
                src_ref=wg_row, dst_ref=wg_all.at[own], send_sem=row_send, recv_sem=row_recv,
                device_id=device(lax.rem(own + off, n_dev)), device_id_type=MESH,
            ).start()

    marginal = total / count
    inside = lanes < bits
    safe = jnp.where(inside, marginal, 0.5)
    plain = safe * jnp.log(safe) + (1.0 - safe) * jnp.log(1.0 - safe)
    neg_codebook = jnp.sum(jnp.where(inside, plain, 0.0), axis=1, keepdims=True)
    ent_all = jnp.sum(jnp.where(lanes == LANES - 1, total, 0.0), axis=1, keepdims=True)
    loss_ref[...] = jnp.broadcast_to(ent_all / count + neg_codebook, (1, LANES))

    ordering.wait()
    wait_bytes(land.at[pl.ds(0, n_dp - 1)], cot_recv)
    odds = log_odds[:bits]
    for k in range(out_slots):
        at = jnp.clip(order_ref[0, k], 0, n_dp * capacity - 1)
        scaled = land[lax.div(at, capacity), pl.ds(lax.rem(at, capacity) * bits, bits), :]
        e = jnp.exp(-jnp.abs(scaled))
        r = 1.0 / (1.0 + e)
        second = 2.0 * (e * r * r * out_mask[k:k + 1, :])
        cot_ref[k] = (-(scaled * second) - second * odds).astype(BF16)

    @pl.when(own < bits)
    def _():
        wait_bytes(wg_all.at[pl.ds(0, bits - 1)], row_recv)
        wait_bytes(wg_own.at[pl.ds(0, bits - 1)], part_send)
        for _ in range(n_dev - 1):
            wait_bytes(wg_row, row_send)

    @pl.when(own >= bits)
    def _():
        wait_bytes(wg_all.at[pl.ds(0, bits)], row_recv)
        wait_bytes(wg_own.at[pl.ds(0, bits)], part_send)

    wg_ref[...] = wg_all[...]
    wait_bytes(stat_all.at[pl.ds(0, n_dev - 1)], stat_send)
    wait_bytes(send_buf.at[pl.ds(0, n_dp - 1)], cot_send)


def local(latents, proj_weight, proj_bias, fill, target, target_slot):
    n_dp = lax.axis_size("dp")
    n_mp = lax.axis_size("mp")
    n_dev = n_dp * n_mp
    width = latents.shape[1]
    bits = proj_weight.shape[0]
    in_slots = latents.shape[0] // BLK
    capacity = max(1, 2 * OUT_SLOTS // n_dp)
    rows = -(-bits // 8) * 8
    chunk_slots = 8
    chunks = in_slots // chunk_slots
    table = (fill.shape[0] // LANES, LANES)
    smem = pltpu.SMEM
    vmem = pl.BlockSpec(memory_space=pltpu.VMEM)
    hbm = pl.BlockSpec(memory_space=pltpu.HBM)
    dma = pltpu.SemaphoreType.DMA
    cot, wg, loss = pl.pallas_call(
        functools.partial(exchange_kernel, n_dp, n_mp, capacity, chunk_slots),
        out_shape=(
            jax.ShapeDtypeStruct((OUT_SLOTS, bits, BLK), BF16),
            jax.ShapeDtypeStruct((bits, 1, width), F32),
            jax.ShapeDtypeStruct((1, LANES), F32),
        ),
        in_specs=[hbm, hbm, hbm, hbm, vmem, vmem],
        out_specs=(vmem, vmem, vmem),
        scratch_shapes=[
            pltpu.VMEM(latents.shape, BF16),
            pltpu.VMEM(table, jnp.int32),
            pltpu.VMEM(table, jnp.int32),
            pltpu.VMEM(table, jnp.int32),
            pltpu.VMEM((in_slots, BLK), F32),
            pltpu.VMEM((OUT_SLOTS, BLK), F32),
            pltpu.VMEM((in_slots, rows, BLK), F32),
            pltpu.VMEM((1, LANES), F32),
            pltpu.VMEM((n_dev, 1, LANES), F32),
            pltpu.VMEM((n_dp, capacity * bits, BLK), F32),
            pltpu.VMEM((n_dp, capacity * bits, BLK), F32),
            pltpu.VMEM((n_dp, in_slots), F32),
            pltpu.VMEM((2, 1, LANES), jnp.int32),
            smem((1, LANES), jnp.int32),
            smem((1, LANES), jnp.int32),
            pltpu.VMEM((bits, 2, width), F32),
            pltpu.VMEM((n_dev, 2, width), F32),
            pltpu.VMEM((1, width), F32),
            pltpu.VMEM((bits, 1, width), F32),
            dma((chunks,)), dma((3,)), dma((2,)), dma(()), dma(()), dma(()), dma(()),
            dma(()), dma(()), dma(()), dma(()),
        ],
        compiler_params=pltpu.CompilerParams(
            collective_id=0, has_side_effects=True, vmem_limit_bytes=67043328
        ),
        name="exchange",
    )(fill.reshape(table), target.reshape(table), target_slot.reshape(table), latents, proj_weight,
      proj_bias.reshape(1, bits))
    grad = jnp.einsum("nbk,bd->nkd", cot, proj_weight, preferred_element_type=F32).astype(BF16)
    return grad.reshape(-1, width), wg.reshape(bits, width), loss[0, 0]


def solution(mesh):
    placed = (P(("dp", "mp"), None), P(), P(), P(), P(), P())
    return jax.shard_map(
        local,
        mesh=mesh,
        in_specs=placed,
        out_specs=(P(("dp", "mp"), None), P(), P()),
        check_vma=False,
    )
```

```python
import functools

import jax
import jax.numpy as jnp
from jax import lax
from jax.experimental import pallas as pl
from jax.experimental.pallas import tpu as pltpu
from jax.sharding import PartitionSpec as P

BLK = 128
OUT_SLOTS = 32
LANES = 128
F32 = jnp.float32
BF16 = jnp.bfloat16
MESH = pl.DeviceIdType.MESH

sharpness = 2.0


def wait_bytes(ref, sem):
    pltpu.make_async_copy(ref, ref, sem).wait()


def to_column(row, rows):
    shape = (rows, row.shape[1])
    diagonal = lax.broadcasted_iota(jnp.int32, shape, 0) == lax.broadcasted_iota(jnp.int32, shape, 1)
    return jnp.sum(jnp.where(diagonal, jnp.broadcast_to(row, shape), 0.0), axis=1, keepdims=True)


def to_row(column):
    shape = (column.shape[0], LANES)
    diagonal = lax.broadcasted_iota(jnp.int32, shape, 0) == lax.broadcasted_iota(jnp.int32, shape, 1)
    return jnp.sum(jnp.where(diagonal, jnp.broadcast_to(column, shape), 0.0), axis=0, keepdims=True)


def slot_row(ref, index, in_slots):
    per = LANES // in_slots
    line = ref[pl.ds(lax.div(index, per), 1), :].astype(F32)
    which = lax.rem(index, per)
    row = line[:, :in_slots]
    for i in range(1, per):
        row = jnp.where(which == i, line[:, i * in_slots:(i + 1) * in_slots], row)
    return row


def exchange_kernel(
    n_dp, n_mp, capacity, chunk_slots,
    fill_hbm, target_hbm, slot_hbm, x_hbm, w_ref, bias_ref,
    cot_ref, wg_ref, loss_ref,
    xbuf, fill_ref, target_ref, slot_ref, mask_ref, first_ref, second_ref, dp_own, dp_all, mp_own, mp_all,
    row_own, row_all, send_buf, land, landed, mine_ref, index_vec, chosen_ref, order_ref,
    x_sem, small_sem, index_sem, dp_send, dp_recv, mp_send, mp_recv, cot_send, cot_recv, row_send, row_recv,
):
    in_slots, rows, _ = first_ref.shape
    depth = dp_own.shape[1]
    bits, width = w_ref.shape
    out_slots = cot_ref.shape[0]
    chunk = chunk_slots * BLK
    chunks = xbuf.shape[0] // chunk
    own_dp = lax.axis_index("dp")
    own_mp = lax.axis_index("mp")
    own = own_dp * n_mp + own_mp
    piece = -(-bits // n_dp)

    def dp_peer(off):
        return {"dp": lax.rem(own_dp + off, n_dp), "mp": own_mp}

    def mp_peer(off):
        return {"dp": own_dp, "mp": lax.rem(own_mp + off, n_mp)}

    def x_copy(c):
        part = pl.ds(c * chunk, chunk)
        return pltpu.make_async_copy(x_hbm.at[part], xbuf.at[part], x_sem.at[c])

    small = [
        pltpu.make_async_copy(src, dst, small_sem.at[i])
        for i, (src, dst) in enumerate(((fill_hbm, fill_ref), (target_hbm, target_ref), (slot_hbm, slot_ref)))
    ]
    for copy in small:
        copy.start()
    for c in range(chunks):
        x_copy(c).start()

    barrier = pltpu.get_barrier_semaphore()

    @pl.loop(1, n_dp)
    def _(off):
        pl.semaphore_signal(barrier, inc=1, device_id=dp_peer(off), device_id_type=MESH)

    @pl.loop(1, n_mp)
    def _(off):
        pl.semaphore_signal(barrier, inc=1, device_id=mp_peer(off), device_id_type=MESH)

    bias = to_column(bias_ref[...], rows)
    w = w_ref[...]
    w = jnp.concatenate([w.astype(F32), jnp.zeros((rows - bits, width), F32)], axis=0).astype(BF16)
    live_row = (lax.broadcasted_iota(jnp.int32, (rows, 1), 0) < bits).astype(F32)
    lanes = lax.broadcasted_iota(jnp.int32, (1, LANES), 1)
    for copy in small:
        copy.wait()

    target_row = slot_row(target_ref, own, in_slots)
    target_col = to_column(target_row, in_slots)
    before = lax.broadcasted_iota(jnp.int32, (in_slots, in_slots), 1) < lax.broadcasted_iota(
        jnp.int32, (in_slots, in_slots), 0
    )
    rank = jnp.sum(jnp.where((target_col == target_row) & before, 1.0, 0.0), axis=1, keepdims=True)
    position = jnp.where(target_col >= 0.0, target_col * float(capacity) + rank, -1.0)
    send_lane = lax.broadcasted_iota(jnp.int32, (in_slots, LANES), 1).astype(F32)
    send_slot = lax.broadcasted_iota(jnp.int32, (in_slots, LANES), 0).astype(F32)
    chosen = jnp.sum(jnp.where(position == send_lane, send_slot, 0.0), axis=0, keepdims=True)
    index_vec[0] = chosen.astype(jnp.int32)
    choose = pltpu.make_async_copy(index_vec.at[0], chosen_ref, index_sem.at[0])
    choose.start()

    fill_col = to_column(slot_row(fill_ref, own, in_slots), in_slots)
    token = lax.broadcasted_iota(jnp.int32, (in_slots, BLK), 1).astype(F32)
    mask_ref[...] = (token < fill_col).astype(F32)
    fills = fill_ref[...].astype(F32)
    count = jnp.sum(jnp.sum(fills, axis=0, keepdims=True), axis=1, keepdims=True)

    def statistics(c, carry):
        bit_acc, ent_acc, both = carry
        x_copy(c).wait()
        x = xbuf[pl.ds(pl.multiple_of(c * chunk, chunk), chunk), :]
        logits = lax.dot_general(w, x, (((1,), (1,)), ((), ())), preferred_element_type=F32) + bias
        scaled = sharpness * logits
        mask = jnp.concatenate(
            [mask_ref[pl.ds(c * chunk_slots + i, 1), :] for i in range(chunk_slots)], axis=1
        )
        size = jnp.abs(scaled)
        e = jnp.exp(-size)
        u = 1.0 + e
        r = 1.0 / u
        er = e * r
        prob = jnp.where(scaled >= 0, r, er) * mask
        ent = (jnp.log(u) + (e - (u - 1.0)) * r + size * er) * mask
        second = 2.0 * (er * r * mask)
        first = -(scaled * second)
        rounded = jnp.concatenate([first, second], axis=0).astype(BF16)
        both = both + jnp.dot(rounded, x, preferred_element_type=F32)
        for i in range(chunk_slots):
            cols = slice(i * BLK, (i + 1) * BLK)
            first_ref[c * chunk_slots + i] = first[:, cols]
            second_ref[c * chunk_slots + i] = second[:, cols]
            bit_acc = bit_acc + prob[:, cols]
            ent_acc = ent_acc + ent[:, cols]
        return bit_acc, ent_acc, both

    zero = jnp.zeros((rows, BLK), F32)
    bit_acc, ent_acc, both = lax.fori_loop(
        0, chunks, statistics, (zero, zero, jnp.zeros((2 * rows, width), F32))
    )
    bit_row = to_row(jnp.sum(bit_acc, axis=1, keepdims=True) * live_row)
    ent_sum = jnp.sum(jnp.sum(ent_acc * live_row, axis=1, keepdims=True), axis=0, keepdims=True)
    stat = jnp.where(lanes == LANES - 1, jnp.broadcast_to(ent_sum, (1, LANES)), bit_row)
    stat = jnp.concatenate([stat, jnp.zeros((1, width - LANES), F32)], axis=1)
    blank = jnp.zeros((1, width), F32)
    for d in range(n_dp):
        mine_bits = [b if b < bits else None for b in range(d * piece, (d + 1) * piece)]
        lines = [blank if b is None else both[b:b + 1] for b in mine_bits]
        lines += [blank if b is None else both[rows + b:rows + b + 1] for b in mine_bits]
        lines += [stat] + [blank] * (depth - 2 * piece - 1)
        dp_own[d] = jnp.concatenate(lines, axis=0)
    dp_all[own_dp] = dp_own[own_dp]
    pl.semaphore_wait(barrier, n_dp + n_mp - 2)

    @pl.loop(1, n_dp)
    def _(off):
        pltpu.make_async_remote_copy(
            src_ref=dp_own.at[lax.rem(own_dp + off, n_dp)], dst_ref=dp_all.at[own_dp],
            send_sem=dp_send, recv_sem=dp_recv, device_id=dp_peer(off), device_id_type=MESH,
        ).start()

    for d in range(n_dp):
        mine_ref[d:d + 1, :] = jnp.where(slot_row(target_ref, d * n_mp + own_mp, in_slots) == own_dp.astype(F32), 1.0, 0.0)
    mine = mine_ref[...]
    later = lax.broadcasted_iota(jnp.int32, (in_slots, in_slots), 0) < lax.broadcasted_iota(
        jnp.int32, (in_slots, in_slots), 1
    )
    ranks = jnp.dot(mine.astype(BF16), later.astype(F32).astype(BF16), preferred_element_type=F32)
    out_index = lax.broadcasted_iota(jnp.int32, (out_slots, in_slots), 0).astype(F32)
    gathered = jnp.zeros((out_slots, in_slots), F32)
    for d in range(n_dp):
        taken = (out_index == slot_row(slot_ref, d * n_mp + own_mp, in_slots)) & (mine[d:d + 1] > 0.0)
        gathered = gathered + jnp.where(taken, float(d * capacity) + ranks[d:d + 1], 0.0)
    index_vec[1] = to_row(jnp.sum(gathered, axis=1, keepdims=True)).astype(jnp.int32)
    ordering = pltpu.make_async_copy(index_vec.at[1], order_ref, index_sem.at[1])
    ordering.start()
    wait_bytes(dp_all.at[pl.ds(0, n_dp - 1)], dp_recv)
    column_sum = jnp.sum(dp_all[...], axis=0)
    mp_own[...] = column_sum
    mp_all[own_mp] = column_sum

    @pl.loop(1, n_mp)
    def _(off):
        pltpu.make_async_remote_copy(
            src_ref=mp_own, dst_ref=mp_all.at[own_mp],
            send_sem=mp_send, recv_sem=mp_recv, device_id=mp_peer(off), device_id_type=MESH,
        ).start()

    choose.wait()
    wait_bytes(mp_all.at[pl.ds(0, n_mp - 1)], mp_recv)
    sums = jnp.sum(mp_all[...], axis=0)
    total = sums[2 * piece:2 * piece + 1, :LANES]
    marginal_c = to_column(total, rows) / count
    log_odds = jnp.log(1.0 - marginal_c) - jnp.log(marginal_c)
    log_odds = jnp.where(live_row > 0, log_odds, 0.0)

    row_index = lax.broadcasted_iota(jnp.int32, (rows, 1), 0)
    lines = []
    for i in range(piece):
        odds = jnp.sum(jnp.where(row_index == own_dp * piece + i, log_odds, 0.0), axis=0, keepdims=True)
        lines.append((sums[i:i + 1] - sums[piece + i:piece + i + 1] * odds) / jnp.sqrt(count))
    finished = jnp.concatenate(lines + [blank] * (row_own.shape[0] - piece), axis=0)
    row_own[...] = finished
    row_all[own_dp] = finished

    @pl.loop(1, n_dp)
    def _(off):
        pltpu.make_async_remote_copy(
            src_ref=row_own, dst_ref=row_all.at[own_dp],
            send_sem=row_send, recv_sem=row_recv, device_id=dp_peer(off), device_id_type=MESH,
        ).start()

    @pl.loop(1, n_dp + 1)
    def _(off):
        peer = lax.rem(own_dp + off, n_dp)
        blocks = []
        for k in range(capacity):
            slot = jnp.clip(chosen_ref[0, peer * capacity + k], 0, in_slots - 1)
            blocks.append((first_ref[slot] - second_ref[slot] * log_odds)[:bits])
        packed = jnp.concatenate(blocks, axis=0).astype(BF16)

        @pl.when(off == n_dp)
        def _():
            land[own_dp] = packed

        @pl.when(off < n_dp)
        def _():
            send_buf[peer] = packed
            pltpu.make_async_remote_copy(
                src_ref=send_buf.at[peer], dst_ref=land.at[own_dp], send_sem=cot_send, recv_sem=cot_recv.at[own_dp],
                device_id=dp_peer(off), device_id_type=MESH,
            ).start()

    marginal = total / count
    inside = lanes < bits
    safe = jnp.where(inside, marginal, 0.5)
    plain = safe * jnp.log(safe) + (1.0 - safe) * jnp.log(1.0 - safe)
    neg_codebook = jnp.sum(jnp.where(inside, plain, 0.0), axis=1, keepdims=True)
    ent_all = jnp.sum(jnp.where(lanes == LANES - 1, total, 0.0), axis=1, keepdims=True)
    loss_ref[...] = jnp.broadcast_to(ent_all / count + neg_codebook, (1, LANES))

    ordering.wait()

    @pl.loop(0, n_dp)
    def _(off):
        src = lax.rem(own_dp + n_dp - off, n_dp)

        @pl.when(off > 0)
        def _():
            wait_bytes(land.at[src], cot_recv.at[src])

        arrived = land[src].astype(F32)
        for k in range(capacity):
            landed[src * capacity + k] = arrived[k * bits:(k + 1) * bits]

    for k in range(out_slots):
        cot_ref[k] = landed[jnp.clip(order_ref[0, k], 0, n_dp * capacity - 1)].astype(BF16)

    wait_bytes(row_all.at[pl.ds(0, n_dp - 1)], row_recv)
    wg_ref[...] = jnp.concatenate([row_all[b // piece, b % piece:b % piece + 1, :] for b in range(bits)], axis=0)
    wait_bytes(dp_own.at[pl.ds(0, n_dp - 1)], dp_send)
    wait_bytes(mp_all.at[pl.ds(0, n_mp - 1)], mp_send)
    wait_bytes(row_all.at[pl.ds(0, n_dp - 1)], row_send)
    wait_bytes(send_buf.at[pl.ds(0, n_dp - 1)], cot_send)


def local(latents, proj_weight, proj_bias, fill, target, target_slot):
    n_dp = lax.axis_size("dp")
    n_mp = lax.axis_size("mp")
    width = latents.shape[1]
    bits = proj_weight.shape[0]
    in_slots = latents.shape[0] // BLK
    capacity = max(1, 2 * OUT_SLOTS // n_dp)
    rows = -(-bits // 8) * 8
    piece = -(-bits // n_dp)
    depth = -(-(2 * piece + 1) // 8) * 8
    row_depth = -(-piece // 8) * 8
    chunk_slots = 8
    chunks = in_slots // chunk_slots
    table = (fill.shape[0] // LANES, LANES)
    smem = pltpu.SMEM
    vmem = pl.BlockSpec(memory_space=pltpu.VMEM)
    hbm = pl.BlockSpec(memory_space=pltpu.HBM)
    dma = pltpu.SemaphoreType.DMA
    cot, wg, loss = pl.pallas_call(
        functools.partial(exchange_kernel, n_dp, n_mp, capacity, chunk_slots),
        out_shape=(
            jax.ShapeDtypeStruct((OUT_SLOTS, bits, BLK), BF16),
            jax.ShapeDtypeStruct((bits, width), F32),
            jax.ShapeDtypeStruct((1, LANES), F32),
        ),
        in_specs=[hbm, hbm, hbm, hbm, vmem, vmem],
        out_specs=(vmem, vmem, vmem),
        scratch_shapes=[
            pltpu.VMEM(latents.shape, BF16),
            pltpu.VMEM(table, jnp.int32),
            pltpu.VMEM(table, jnp.int32),
            pltpu.VMEM(table, jnp.int32),
            pltpu.VMEM((in_slots, BLK), F32),
            pltpu.VMEM((in_slots, rows, BLK), F32),
            pltpu.VMEM((in_slots, rows, BLK), F32),
            pltpu.VMEM((n_dp, depth, width), F32),
            pltpu.VMEM((n_dp, depth, width), F32),
            pltpu.VMEM((depth, width), F32),
            pltpu.VMEM((n_mp, depth, width), F32),
            pltpu.VMEM((row_depth, width), F32),
            pltpu.VMEM((n_dp, row_depth, width), F32),
            pltpu.VMEM((n_dp, capacity * bits, BLK), BF16),
            pltpu.VMEM((n_dp, capacity * bits, BLK), BF16),
            pltpu.VMEM((n_dp * capacity, bits, BLK), F32),
            pltpu.VMEM((n_dp, in_slots), F32),
            pltpu.VMEM((2, 1, LANES), jnp.int32),
            smem((1, LANES), jnp.int32),
            smem((1, LANES), jnp.int32),
            dma((chunks,)), dma((3,)), dma((2,)), dma(()), dma(()), dma(()), dma(()),
            dma(()), dma((n_dp,)), dma(()), dma(()),
        ],
        compiler_params=pltpu.CompilerParams(
            collective_id=0, has_side_effects=True, vmem_limit_bytes=67043328
        ),
        name="exchange",
    )(fill.reshape(table), target.reshape(table), target_slot.reshape(table), latents, proj_weight,
      proj_bias.reshape(1, bits))
    grad = jnp.einsum("nbk,bd->nkd", cot, proj_weight, preferred_element_type=F32).astype(BF16)
    return grad.reshape(-1, width), wg, loss[0, 0]


def solution(mesh):
    placed = (P(("dp", "mp"), None), P(), P(), P(), P(), P())
    return jax.shard_map(
        local,
        mesh=mesh,
        in_specs=placed,
        out_specs=(P(("dp", "mp"), None), P(), P()),
        check_vma=False,
    )
```
